128 devices in a mesh: seq: 32 (over z, y_lo, x), grp: 4 (over y_hi, core).
Axes of the slice: x: 4, y: 4 (y_hi: 2, y_lo: 2; y = y_hi * 2 + y_lo), z: 4, core: 2. Of those that a mesh axis runs over, the one named last changes fastest.
Arguments:
- queries: bfloat16 [32768, 4096], P(('grp', 'seq')), parts along dimension 0, may hold values from -6 to 6
- stored_keys: bfloat16 [32768, 2048], P(('grp', 'seq')), parts along dimension 0, may hold values from -6 to 6
- stored_values: bfloat16 [32768, 2048], P(('grp', 'seq')), parts along dimension 0, may hold values from -6 to 6
- stored_output: bfloat16 [32768, 4096], P(('grp', 'seq')), parts along dimension 0, may hold values from -6 to 6
- output_cotangent: bfloat16 [32768, 4096], P(('grp', 'seq')), parts along dimension 0, may hold values from -48 to 48
- score_logsumexp: float32 [32, 32768], P(None, ('grp', 'seq')), parts along dimension 1, may hold values from 6.5 to 7.5
- valid_count: int32 [4], P('grp'), parts along dimension 0, may hold values from 4096 to 8192
Outputs:
- query_gradient: float32 [32768, 4096], P(('grp', 'seq')), parts along dimension 0
- key_grad: float32 [32768, 2048], P(('grp', 'seq')), parts along dimension 0
- value_grad: float32 [32768, 2048], P(('grp', 'seq')), parts along dimension 0
The draws below stay inside these ranges and needn't reach their ends.
There are 4 independent parts, one for each index of `grp`. The reference program is written for one: setup_inputs(seed, part) draws one part's arguments, and reference() takes and returns one part's arrays. A program takes and returns all parts, laid end to end along the dimension named above; each array names one. Nothing has to cross between parts.
All inputs are finite; a program needn't handle non-finite values.
Results may differ from the reference program's by a relative error of at most 0.0047.
Values may be sent and summed in bfloat16 or wider, within the bound.
A program may use at most 128 MiB of HBM per device.

```python
import jax
import jax.numpy as jnp
from jax import lax

QUERY_HEADS = 32
KEY_VALUE_HEADS = 16
HEAD_SIZE = 128
WINDOW = 1024
TOK_DEV = 256
WINDOW_TOKENS = 8192
N_SEQ = 32


def block_levels(stream_key, extent, split, least, largest):
    loudness = 1.0
    for axis_at, parts in split:
        steps = jax.random.uniform(jax.random.fold_in(jax.random.fold_in(stream_key, 6), axis_at), (parts,), jnp.float32, least / len(split), largest / len(split))
        loudness = loudness * jnp.repeat(jnp.exp(steps), extent[axis_at] // parts).reshape((-1,) + (1,) * (len(extent) - 1 - axis_at))
    return loudness


def gaussian(key, dims, width, most, split=(), kind=jnp.bfloat16):
    entries = width * jax.random.normal(key, dims, jnp.float32)
    if split:
        entries = entries * block_levels(key, dims, split, -0.22, 0.18)
    return jnp.clip(entries, -most, most).astype(kind)


def setup_inputs(seed: int = 0, part: int = 0) -> dict:
    arg_keys = jax.random.split(jax.random.key(seed), 8)
    own_keys = jax.random.split(jax.random.fold_in(arg_keys[7], part), 8)
    queries = gaussian(own_keys[0], (WINDOW_TOKENS, QUERY_HEADS * HEAD_SIZE), 1.0, 6.0, ((0, 32),))
    stored_keys = gaussian(own_keys[1], (WINDOW_TOKENS, KEY_VALUE_HEADS * HEAD_SIZE), 1.0, 6.0, ((0, 32),))
    stored_values = gaussian(own_keys[2], (WINDOW_TOKENS, KEY_VALUE_HEADS * HEAD_SIZE), 1.0, 6.0, ((0, 32),))
    stored_output = gaussian(own_keys[3], (WINDOW_TOKENS, QUERY_HEADS * HEAD_SIZE), 1.0, 6.0, ((0, 32),))
    output_cotangent = gaussian(own_keys[4], (WINDOW_TOKENS, QUERY_HEADS * HEAD_SIZE), 8.0, 48.0, ((0, 32),))
    score_logsumexp = jnp.clip(6.5 + 1.0 * jax.random.uniform(own_keys[5], (QUERY_HEADS, WINDOW_TOKENS), jnp.float32) ** block_levels(own_keys[5], (QUERY_HEADS, WINDOW_TOKENS), ((1, 32),), -0.2, 0.2), 6.5, 7.5)
    valid_count = jax.random.randint(own_keys[6], (1,), WINDOW_TOKENS // 2, WINDOW_TOKENS + 1).astype(jnp.int32)
    return dict(queries=queries, stored_keys=stored_keys, stored_values=stored_values, stored_output=stored_output, output_cotangent=output_cotangent, score_logsumexp=score_logsumexp, valid_count=valid_count)


score_scale = 168.0 ** -0.5


def reference(queries, stored_keys, stored_values, stored_output, output_cotangent, score_logsumexp, valid_count):
    head_group = QUERY_HEADS // KEY_VALUE_HEADS
    blocks = WINDOW // TOK_DEV
    window_span = (blocks + 1) * TOK_DEV
    window_margin = blocks * TOK_DEV
    empty_rows = jnp.zeros((window_margin, KEY_VALUE_HEADS * HEAD_SIZE), jnp.bfloat16)
    key_padded = jnp.concatenate([empty_rows, stored_keys], 0)
    value_padded = jnp.concatenate([empty_rows, stored_values], 0)
    query_quad = queries.reshape(WINDOW_TOKENS, KEY_VALUE_HEADS, head_group, HEAD_SIZE)
    gradient_quad = output_cotangent.reshape(WINDOW_TOKENS, KEY_VALUE_HEADS, head_group, HEAD_SIZE)
    delta_total = jnp.sum(output_cotangent.reshape(WINDOW_TOKENS, KEY_VALUE_HEADS, head_group, HEAD_SIZE).astype(jnp.float32)
                        * stored_output.reshape(WINDOW_TOKENS, KEY_VALUE_HEADS, head_group, HEAD_SIZE).astype(jnp.float32), -1)
    logsumexp_quad = score_logsumexp.T.reshape(WINDOW_TOKENS, KEY_VALUE_HEADS, head_group)
    limit = valid_count[0]

    def block_step(carry, block_idx):
        key_gradient_total, value_gradient_total = carry
        start_offset = (block_idx * TOK_DEV).astype(jnp.int32)
        query_blk = lax.dynamic_slice_in_dim(query_quad, start_offset, TOK_DEV, 0).astype(jnp.float32)
        grad_blk = lax.dynamic_slice_in_dim(gradient_quad, start_offset, TOK_DEV, 0).astype(jnp.float32)
        key_block_rows = lax.dynamic_slice_in_dim(key_padded, start_offset, window_span, 0).reshape(window_span, KEY_VALUE_HEADS, HEAD_SIZE).astype(jnp.float32)
        value_block_rows = lax.dynamic_slice_in_dim(value_padded, start_offset, window_span, 0).reshape(window_span, KEY_VALUE_HEADS, HEAD_SIZE).astype(jnp.float32)
        lse_blk = jnp.transpose(lax.dynamic_slice_in_dim(logsumexp_quad, start_offset, TOK_DEV, 0), (1, 2, 0))
        delta_blk = jnp.transpose(lax.dynamic_slice_in_dim(delta_total, start_offset, TOK_DEV, 0), (1, 2, 0))
        query_pos = start_offset + jnp.arange(TOK_DEV, dtype=jnp.int32)
        key_pos = start_offset - window_margin + jnp.arange(window_span, dtype=jnp.int32)
        live = ((key_pos[None, :] <= query_pos[:, None]) & (query_pos[:, None] - key_pos[None, :] < WINDOW)
                & (key_pos[None, :] >= 0) & (query_pos[:, None] < limit) & (key_pos[None, :] < limit))
        scores = jnp.einsum('ihgd,jhd->hgij', query_blk, key_block_rows) * score_scale
        probs = jnp.where(live[None, None], jnp.exp(scores - lse_blk[..., None]), 0.0)
        probs_b = lax.optimization_barrier(probs.astype(jnp.bfloat16)).astype(jnp.float32)
        value_piece = jnp.einsum('hgij,ihgd->jhd', probs_b, grad_blk)
        dprobs = jnp.einsum('ihgd,jhd->hgij', grad_blk, value_block_rows)
        dscores = lax.optimization_barrier((probs * (dprobs - delta_blk[..., None])).astype(jnp.bfloat16)).astype(jnp.float32)
        query_part = jnp.einsum('hgij,jhd->ihgd', dscores, key_block_rows) * score_scale
        key_piece = jnp.einsum('hgij,ihgd->jhd', dscores, query_blk) * score_scale
        previous_key = lax.dynamic_slice_in_dim(key_gradient_total, start_offset, window_span, 0)
        previous_value = lax.dynamic_slice_in_dim(value_gradient_total, start_offset, window_span, 0)
        key_gradient_total = lax.dynamic_update_slice_in_dim(key_gradient_total, previous_key + key_piece.reshape(window_span, KEY_VALUE_HEADS * HEAD_SIZE), start_offset, 0)
        value_gradient_total = lax.dynamic_update_slice_in_dim(value_gradient_total, previous_value + value_piece.reshape(window_span, KEY_VALUE_HEADS * HEAD_SIZE), start_offset, 0)
        return (key_gradient_total, value_gradient_total), query_part.reshape(TOK_DEV, QUERY_HEADS * HEAD_SIZE)

    start_offset_total = (jnp.zeros((window_margin + WINDOW_TOKENS, KEY_VALUE_HEADS * HEAD_SIZE), jnp.float32),
                 jnp.zeros((window_margin + WINDOW_TOKENS, KEY_VALUE_HEADS * HEAD_SIZE), jnp.float32))
    (key_gradient_total, value_gradient_total), query_parts = lax.scan(block_step, start_offset_total, jnp.arange(N_SEQ, dtype=jnp.int32))
    return query_parts.reshape(WINDOW_TOKENS, QUERY_HEADS * HEAD_SIZE), key_gradient_total[window_margin:], value_gradient_total[window_margin:]
```

```python
import functools

import jax
import jax.numpy as jnp
from jax import lax
from jax.experimental import pallas as pl
from jax.experimental.pallas import tpu as pltpu
from jax.sharding import PartitionSpec as P

QUERY_HEADS = 32
KEY_VALUE_HEADS = 16
HEAD_SIZE = 128
WINDOW = 1024


score_scale = 168.0 ** (-0.5)


def passed_along(x, axis, by):
    count = lax.axis_size(axis)
    pairs = [(i, i + by) for i in range(count) if 0 <= i + by < count]
    return lax.ppermute(x, axis, pairs)


def pair_kernel(group, accumulate, sc_ref, q_ref, do_ref, k_ref, v_ref, lse_ref, dl_ref, *rest):
    if accumulate:
        dq_in_ref, dq_ref, dk_ref, dv_ref = rest
    else:
        dq_ref, dk_ref, dv_ref = rest
    rows = q_ref.shape[0]
    cols = k_ref.shape[0]
    qs = sc_ref[0]
    ks = sc_ref[1]
    vc = sc_ref[2]
    i = lax.broadcasted_iota(jnp.int32, (rows, cols), 0) + qs
    j = lax.broadcasted_iota(jnp.int32, (rows, cols), 1) + ks
    live = (j <= i) & (i - j < WINDOW) & (j >= 0) & (i < vc) & (j < vc)
    k = k_ref[...]
    v = v_ref[...]
    dk = jnp.zeros((cols, HEAD_SIZE), jnp.float32)
    dv = jnp.zeros((cols, HEAD_SIZE), jnp.float32)
    nt = (((1,), (1,)), ((), ()))
    tn = (((0,), (0,)), ((), ()))
    for g in range(group):
        sl = slice(g * HEAD_SIZE, (g + 1) * HEAD_SIZE)
        q = q_ref[:, sl]
        do = do_ref[:, sl]
        lse = lse_ref[0, :, g : g + 1]
        dl = dl_ref[0, :, g : g + 1]
        s = lax.dot_general(q, k, nt, preferred_element_type=jnp.float32) * score_scale
        p = jnp.where(live, jnp.exp(s - lse), 0.0)
        dp = lax.dot_general(do, v, nt, preferred_element_type=jnp.float32)
        ds = (p * (dp - dl)).astype(jnp.bfloat16)
        pb = p.astype(jnp.bfloat16)
        dv = dv + lax.dot_general(pb, do, tn, preferred_element_type=jnp.float32)
        dk = dk + lax.dot_general(ds, q, tn, preferred_element_type=jnp.float32)
        dq = jnp.dot(ds, k, preferred_element_type=jnp.float32) * score_scale
        if accumulate:
            dq = dq + dq_in_ref[:, sl]
        dq_ref[:, sl] = dq
    dk_ref[...] = (dk * score_scale).astype(dk_ref.dtype)
    dv_ref[...] = dv.astype(dv_ref.dtype)


def pair_grads(scalars, q, do, k, v, lse3, dl3, dq_in, kv_dtype):
    rows = q.shape[0]
    cols = k.shape[0]
    group = QUERY_HEADS // KEY_VALUE_HEADS
    accumulate = dq_in is not None
    qspec = pl.BlockSpec((rows, group * HEAD_SIZE), lambda h, sc: (0, h))
    kspec = pl.BlockSpec((cols, HEAD_SIZE), lambda h, sc: (0, h))
    sspec = pl.BlockSpec((1, rows, group), lambda h, sc: (h, 0, 0))
    in_specs = [qspec, qspec, kspec, kspec, sspec, sspec]
    args = [q, do, k, v, lse3, dl3]
    if accumulate:
        in_specs.append(qspec)
        args.append(dq_in)
    out_shape = (
        jax.ShapeDtypeStruct((rows, QUERY_HEADS * HEAD_SIZE), jnp.float32),
        jax.ShapeDtypeStruct((cols, KEY_VALUE_HEADS * HEAD_SIZE), kv_dtype),
        jax.ShapeDtypeStruct((cols, KEY_VALUE_HEADS * HEAD_SIZE), kv_dtype),
    )
    flops = 5 * 2 * rows * cols * HEAD_SIZE * QUERY_HEADS
    nbytes = 2 * (2 * q.size + 2 * k.size) + 4 * q.size * (2 if accumulate else 1) + 2 * 2 * k.size * jnp.dtype(kv_dtype).itemsize
    return pl.pallas_call(
        functools.partial(pair_kernel, group, accumulate),
        out_shape=out_shape,
        grid_spec=pltpu.PrefetchScalarGridSpec(
            num_scalar_prefetch=1,
            grid=(KEY_VALUE_HEADS,),
            in_specs=in_specs,
            out_specs=[qspec, kspec, kspec],
        ),
        input_output_aliases=({7: 0} if accumulate else {}),
        cost_estimate=pl.CostEstimate(
            flops=flops, transcendentals=rows * cols * QUERY_HEADS, bytes_accessed=int(nbytes)
        ),
    )(scalars, *args)


def local(
    queries,
    stored_keys,
    stored_values,
    stored_output,
    output_cotangent,
    score_logsumexp,
    valid_count,
):
    tokens_here = queries.shape[0]
    blocks = WINDOW // tokens_here
    group = QUERY_HEADS // KEY_VALUE_HEADS
    shard = lax.axis_index("seq")
    halos = []
    for distance in range(1, blocks + 1):
        halos.append(passed_along((stored_keys, stored_values), "seq", distance))
    limit = valid_count[0]

    delta = jnp.sum(
        (output_cotangent.astype(jnp.float32) * stored_output.astype(jnp.float32)).reshape(
            tokens_here, QUERY_HEADS, HEAD_SIZE
        ),
        -1,
    )
    dl3 = delta.reshape(tokens_here, KEY_VALUE_HEADS, group).transpose(1, 0, 2)
    lse3 = score_logsumexp.T.reshape(tokens_here, KEY_VALUE_HEADS, group).transpose(1, 0, 2)
    qstart = shard * tokens_here

    def scalars_for(distance):
        return jnp.stack([qstart, qstart - distance * tokens_here, limit]).astype(jnp.int32)

    dq, key_grad, value_grad = pair_grads(
        scalars_for(0), queries, output_cotangent, stored_keys, stored_values, lse3, dl3, None, jnp.float32
    )
    for distance in range(1, blocks + 1):
        k_far, v_far = halos[distance - 1]
        dq, dk_part, dv_part = pair_grads(
            scalars_for(distance),
            queries,
            output_cotangent,
            k_far,
            v_far,
            lse3,
            dl3,
            dq,
            jnp.bfloat16,
        )
        arrived = passed_along((dk_part, dv_part), "seq", -distance)
        key_grad = key_grad + arrived[0].astype(jnp.float32)
        value_grad = value_grad + arrived[1].astype(jnp.float32)
    return (dq, key_grad, value_grad)


def solution(mesh):
    placed = (
        P(("grp", "seq"), None),
        P(("grp", "seq"), None),
        P(("grp", "seq"), None),
        P(("grp", "seq"), None),
        P(("grp", "seq"), None),
        P(None, ("grp", "seq")),
        P("grp"),
    )
    return jax.shard_map(
        local,
        mesh=mesh,
        in_specs=placed,
        out_specs=(P(("grp", "seq"), None), P(("grp", "seq"), None), P(("grp", "seq"), None)),
        check_vma=False,
    )
```

```python
import functools

import jax
import jax.numpy as jnp
from jax import lax
from jax.experimental import pallas as pl
from jax.experimental.pallas import tpu as pltpu
from jax.sharding import PartitionSpec as P


QUERY_HEADS = 32
KEY_VALUE_HEADS = 16
HEAD_SIZE = 128
WINDOW = 1024
HEADS_PER_STEP = 4


score_scale = 168.0 ** (-0.5)


def passed_along(x, axis, by):
    count = lax.axis_size(axis)
    pairs = [(i, i + by) for i in range(count) if 0 <= i + by < count]
    return lax.ppermute(x, axis, pairs)


def pair_kernel(group, heads, accumulate, sc_ref, q_ref, do_ref, k_ref, v_ref, lse_ref, dl_ref, *rest):
    if accumulate:
        dq_in_ref, dq_ref, dk_ref, dv_ref = rest
    else:
        dq_ref, dk_ref, dv_ref = rest
    rows = q_ref.shape[0]
    cols = k_ref.shape[0]
    qs = sc_ref[0]
    ks = sc_ref[1]
    vc = sc_ref[2]
    i = lax.broadcasted_iota(jnp.int32, (rows, cols), 0) + qs
    j = lax.broadcasted_iota(jnp.int32, (rows, cols), 1) + ks
    live = (j <= i) & (i - j < WINDOW) & (j >= 0) & (i < vc) & (j < vc)
    nt = (((1,), (1,)), ((), ()))
    tn = (((0,), (0,)), ((), ()))
    for c in range(heads):
        ksl = slice(c * HEAD_SIZE, (c + 1) * HEAD_SIZE)
        k = k_ref[:, ksl]
        v = v_ref[:, ksl]
        dk = jnp.zeros((cols, HEAD_SIZE), jnp.float32)
        dv = jnp.zeros((cols, HEAD_SIZE), jnp.float32)
        for g in range(group):
            hq = c * group + g
            sl = slice(hq * HEAD_SIZE, (hq + 1) * HEAD_SIZE)
            q = q_ref[:, sl]
            do = do_ref[:, sl]
            lse = lse_ref[c, :, g : g + 1]
            dl = dl_ref[c, :, g : g + 1]
            s = lax.dot_general(q, k, nt, preferred_element_type=jnp.float32) * score_scale
            p = jnp.where(live, jnp.exp(s - lse), 0.0)
            dp = lax.dot_general(do, v, nt, preferred_element_type=jnp.float32)
            ds = (p * (dp - dl)).astype(jnp.bfloat16)
            pb = p.astype(jnp.bfloat16)
            dv = dv + lax.dot_general(pb, do, tn, preferred_element_type=jnp.float32)
            dk = dk + lax.dot_general(ds, q, tn, preferred_element_type=jnp.float32)
            dq = jnp.dot(ds, k, preferred_element_type=jnp.float32) * score_scale
            if accumulate:
                dq = dq + dq_in_ref[:, sl]
            dq_ref[:, sl] = dq
        dk_ref[:, ksl] = (dk * score_scale).astype(dk_ref.dtype)
        dv_ref[:, ksl] = dv.astype(dv_ref.dtype)


def pair_grads(scalars, q, do, k, v, lse3, dl3, dq_in, kv_dtype):
    rows = q.shape[0]
    cols = k.shape[0]
    group = QUERY_HEADS // KEY_VALUE_HEADS
    accumulate = dq_in is not None
    heads = HEADS_PER_STEP
    qspec = pl.BlockSpec((rows, heads * group * HEAD_SIZE), lambda h, sc: (0, h))
    kspec = pl.BlockSpec((cols, heads * HEAD_SIZE), lambda h, sc: (0, h))
    sspec = pl.BlockSpec((heads, rows, group), lambda h, sc: (h, 0, 0))
    in_specs = [qspec, qspec, kspec, kspec, sspec, sspec]
    args = [q, do, k, v, lse3, dl3]
    if accumulate:
        in_specs.append(qspec)
        args.append(dq_in)
    out_shape = (
        jax.ShapeDtypeStruct((rows, QUERY_HEADS * HEAD_SIZE), jnp.float32),
        jax.ShapeDtypeStruct((cols, KEY_VALUE_HEADS * HEAD_SIZE), kv_dtype),
        jax.ShapeDtypeStruct((cols, KEY_VALUE_HEADS * HEAD_SIZE), kv_dtype),
    )
    flops = 5 * 2 * rows * cols * HEAD_SIZE * QUERY_HEADS
    nbytes = 2 * (2 * q.size + 2 * k.size) + 4 * q.size * (2 if accumulate else 1) + 2 * 2 * k.size * jnp.dtype(kv_dtype).itemsize
    return pl.pallas_call(
        functools.partial(pair_kernel, group, heads, accumulate),
        out_shape=out_shape,
        grid_spec=pltpu.PrefetchScalarGridSpec(
            num_scalar_prefetch=1,
            grid=(KEY_VALUE_HEADS // heads,),
            in_specs=in_specs,
            out_specs=[qspec, kspec, kspec],
        ),
        input_output_aliases=({7: 0} if accumulate else {}),
        cost_estimate=pl.CostEstimate(
            flops=flops, transcendentals=rows * cols * QUERY_HEADS, bytes_accessed=int(nbytes)
        ),
    )(scalars, *args)


def local(
    queries,
    stored_keys,
    stored_values,
    stored_output,
    output_cotangent,
    score_logsumexp,
    valid_count,
):
    tokens_here = queries.shape[0]
    blocks = WINDOW // tokens_here
    group = QUERY_HEADS // KEY_VALUE_HEADS
    shard = lax.axis_index("seq")
    halos = []
    for distance in range(1, blocks + 1):
        halos.append(passed_along((stored_keys, stored_values), "seq", distance))
    limit = valid_count[0]

    delta = jnp.sum(
        (output_cotangent.astype(jnp.float32) * stored_output.astype(jnp.float32)).reshape(
            tokens_here, QUERY_HEADS, HEAD_SIZE
        ),
        -1,
    )
    dl3 = delta.reshape(tokens_here, KEY_VALUE_HEADS, group).transpose(1, 0, 2)
    lse3 = score_logsumexp.T.reshape(tokens_here, KEY_VALUE_HEADS, group).transpose(1, 0, 2)
    qstart = shard * tokens_here

    def scalars_for(distance):
        return jnp.stack([qstart, qstart - distance * tokens_here, limit]).astype(jnp.int32)

    dq, key_grad, value_grad = pair_grads(
        scalars_for(0), queries, output_cotangent, stored_keys, stored_values, lse3, dl3, None, jnp.float32
    )
    for distance in range(1, blocks + 1):
        k_far, v_far = halos[distance - 1]
        dq, dk_part, dv_part = pair_grads(
            scalars_for(distance),
            queries,
            output_cotangent,
            k_far,
            v_far,
            lse3,
            dl3,
            dq,
            jnp.bfloat16,
        )
        arrived = passed_along((dk_part, dv_part), "seq", -distance)
        key_grad = key_grad + arrived[0].astype(jnp.float32)
        value_grad = value_grad + arrived[1].astype(jnp.float32)
    return (dq, key_grad, value_grad)


def solution(mesh):
    placed = (
        P(("grp", "seq"), None),
        P(("grp", "seq"), None),
        P(("grp", "seq"), None),
        P(("grp", "seq"), None),
        P(("grp", "seq"), None),
        P(None, ("grp", "seq")),
        P("grp"),
    )

    return jax.shard_map(
        local,
        mesh=mesh,
        in_specs=placed,
        out_specs=(P(("grp", "seq"), None), P(("grp", "seq"), None), P(("grp", "seq"), None)),
        check_vma=False,
    )
```

```python
import functools

import jax
import jax.numpy as jnp
from jax import lax
from jax.experimental import pallas as pl
from jax.experimental.pallas import tpu as pltpu
from jax.sharding import PartitionSpec as P


QUERY_HEADS = 32
KEY_VALUE_HEADS = 16
HEAD_SIZE = 128
WINDOW = 1024
HEADS_PER_STEP = 4
ROW_DEVICES = 4
PAIR_ORDER = (1, 4, 2, 3)


score_scale = 168.0 ** (-0.5)


def passed_along(x, axis, by):
    count = lax.axis_size(axis)
    pairs = [(i, i + by) for i in range(count) if 0 <= i + by < count]
    return lax.ppermute(x, axis, pairs)


def pair_kernel(group, heads, accumulate, sc_ref, q_ref, do_ref, k_ref, v_ref, lse_ref, dl_ref, *rest):
    if accumulate:
        dq_in_ref, dq_ref, dk_ref, dv_ref = rest
    else:
        dq_ref, dk_ref, dv_ref = rest
    rows = q_ref.shape[0]
    cols = k_ref.shape[0]
    qs = sc_ref[0]
    ks = sc_ref[1]
    vc = sc_ref[2]
    i = lax.broadcasted_iota(jnp.int32, (rows, cols), 0) + qs
    j = lax.broadcasted_iota(jnp.int32, (rows, cols), 1) + ks
    live = (j <= i) & (i - j < WINDOW) & (j >= 0) & (i < vc) & (j < vc)
    nt = (((1,), (1,)), ((), ()))
    tn = (((0,), (0,)), ((), ()))
    for c in range(heads):
        ksl = slice(c * HEAD_SIZE, (c + 1) * HEAD_SIZE)
        k = k_ref[:, ksl]
        v = v_ref[:, ksl]
        dk = jnp.zeros((cols, HEAD_SIZE), jnp.float32)
        dv = jnp.zeros((cols, HEAD_SIZE), jnp.float32)
        for g in range(group):
            hq = c * group + g
            sl = slice(hq * HEAD_SIZE, (hq + 1) * HEAD_SIZE)
            q = q_ref[:, sl]
            do = do_ref[:, sl]
            lse = lse_ref[c, :, g : g + 1]
            dl = dl_ref[c, :, g : g + 1]
            s = lax.dot_general(q, k, nt, preferred_element_type=jnp.float32) * score_scale
            p = jnp.where(live, jnp.exp(s - lse), 0.0)
            dp = lax.dot_general(do, v, nt, preferred_element_type=jnp.float32)
            ds = (p * (dp - dl)).astype(jnp.bfloat16)
            pb = p.astype(jnp.bfloat16)
            dv = dv + lax.dot_general(pb, do, tn, preferred_element_type=jnp.float32)
            dk = dk + lax.dot_general(ds, q, tn, preferred_element_type=jnp.float32)
            dq = jnp.dot(ds, k, preferred_element_type=jnp.float32) * score_scale
            if accumulate:
                dq = dq + dq_in_ref[:, sl]
            dq_ref[:, sl] = dq
        dk_ref[:, ksl] = (dk * score_scale).astype(dk_ref.dtype)
        dv_ref[:, ksl] = dv.astype(dv_ref.dtype)


def pair_grads(scalars, q, do, k, v, lse3, dl3, dq_in, kv_dtype):
    rows = q.shape[0]
    cols = k.shape[0]
    group = QUERY_HEADS // KEY_VALUE_HEADS
    accumulate = dq_in is not None
    heads = HEADS_PER_STEP
    qspec = pl.BlockSpec((rows, heads * group * HEAD_SIZE), lambda h, sc: (0, h))
    kspec = pl.BlockSpec((cols, heads * HEAD_SIZE), lambda h, sc: (0, h))
    sspec = pl.BlockSpec((heads, rows, group), lambda h, sc: (h, 0, 0))
    in_specs = [qspec, qspec, kspec, kspec, sspec, sspec]
    args = [q, do, k, v, lse3, dl3]
    if accumulate:
        in_specs.append(qspec)
        args.append(dq_in)
    out_shape = (
        jax.ShapeDtypeStruct((rows, QUERY_HEADS * HEAD_SIZE), jnp.float32),
        jax.ShapeDtypeStruct((cols, KEY_VALUE_HEADS * HEAD_SIZE), kv_dtype),
        jax.ShapeDtypeStruct((cols, KEY_VALUE_HEADS * HEAD_SIZE), kv_dtype),
    )
    flops = 5 * 2 * rows * cols * HEAD_SIZE * QUERY_HEADS
    nbytes = 2 * (2 * q.size + 2 * k.size) + 4 * q.size * (2 if accumulate else 1) + 2 * 2 * k.size * jnp.dtype(kv_dtype).itemsize
    return pl.pallas_call(
        functools.partial(pair_kernel, group, heads, accumulate),
        out_shape=out_shape,
        grid_spec=pltpu.PrefetchScalarGridSpec(
            num_scalar_prefetch=1,
            grid=(KEY_VALUE_HEADS // heads,),
            in_specs=in_specs,
            out_specs=[qspec, kspec, kspec],
        ),
        input_output_aliases=({7: 0} if accumulate else {}),
        cost_estimate=pl.CostEstimate(
            flops=flops, transcendentals=rows * cols * QUERY_HEADS, bytes_accessed=int(nbytes)
        ),
    )(scalars, *args)


def sent_by(x, axis, pairs):
    return lax.ppermute(x, axis, pairs)


def local(
    queries,
    stored_keys,
    stored_values,
    stored_output,
    output_cotangent,
    score_logsumexp,
    valid_count,
):
    tokens_here = queries.shape[0]
    blocks = WINDOW // tokens_here
    group = QUERY_HEADS // KEY_VALUE_HEADS
    count = lax.axis_size("seq")
    shard = lax.axis_index("seq")
    row = ROW_DEVICES
    kv = (stored_keys, stored_values)
    far = passed_along(kv, "seq", blocks)
    near = sent_by(kv, "seq", [(i, i + 1) for i in range(count - 1) if i % row != row - 1])
    handed = sent_by(far, "seq", [(i, i - row + 1) for i in range(row, count) if i % row == row - 1])
    halos = {blocks: far, 1: (near[0] + handed[0], near[1] + handed[1])}
    for distance in range(2, blocks):
        halos[distance] = passed_along(kv, "seq", distance)
    limit = valid_count[0]

    delta = jnp.sum(
        (output_cotangent.astype(jnp.float32) * stored_output.astype(jnp.float32)).reshape(
            tokens_here, QUERY_HEADS, HEAD_SIZE
        ),
        -1,
    )
    dl3 = delta.reshape(tokens_here, KEY_VALUE_HEADS, group).transpose(1, 0, 2)
    lse3 = score_logsumexp.T.reshape(tokens_here, KEY_VALUE_HEADS, group).transpose(1, 0, 2)
    qstart = shard * tokens_here

    def scalars_for(distance):
        return jnp.stack([qstart, qstart - distance * tokens_here, limit]).astype(jnp.int32)

    dq, key_grad, value_grad = pair_grads(
        scalars_for(0), queries, output_cotangent, stored_keys, stored_values, lse3, dl3, None, jnp.float32
    )
    handed_back = None
    for distance in PAIR_ORDER:
        k_far, v_far = halos[distance]
        dq, dk_part, dv_part = pair_grads(
            scalars_for(distance),
            queries,
            output_cotangent,
            k_far,
            v_far,
            lse3,
            dl3,
            dq,
            jnp.bfloat16,
        )
        if distance == 1:
            arrived = sent_by(
                (dk_part, dv_part), "seq", [(i, i - 1) for i in range(1, count) if i % row != 0]
            )
            handed_back = sent_by(
                (dk_part, dv_part), "seq", [(i, i + row - 1) for i in range(row, count) if i % row == 0]
            )
        else:
            if distance == blocks:
                dk_part = (dk_part.astype(jnp.float32) + handed_back[0].astype(jnp.float32)).astype(jnp.bfloat16)
                dv_part = (dv_part.astype(jnp.float32) + handed_back[1].astype(jnp.float32)).astype(jnp.bfloat16)
            arrived = passed_along((dk_part, dv_part), "seq", -distance)
        key_grad = key_grad + arrived[0].astype(jnp.float32)
        value_grad = value_grad + arrived[1].astype(jnp.float32)
    return (dq, key_grad, value_grad)


def solution(mesh):
    placed = (
        P(("grp", "seq"), None),
        P(("grp", "seq"), None),
        P(("grp", "seq"), None),
        P(("grp", "seq"), None),
        P(("grp", "seq"), None),
        P(None, ("grp", "seq")),
        P("grp"),
    )

    return jax.shard_map(
        local,
        mesh=mesh,
        in_specs=placed,
        out_specs=(P(("grp", "seq"), None), P(("grp", "seq"), None), P(("grp", "seq"), None)),
        check_vma=False,
    )
```

```python
import functools

import jax
import jax.numpy as jnp
from jax import lax
from jax.experimental import pallas as pl
from jax.experimental.pallas import tpu as pltpu
from jax.sharding import PartitionSpec as P


QUERY_HEADS = 32
KEY_VALUE_HEADS = 16
HEAD_SIZE = 128
WINDOW = 1024
HEADS_PER_STEP = 4
ROW_DEVICES = 4
PAIR_ORDER = (1, 4, 2, 3)


score_scale = 168.0 ** (-0.5)


def passed_along(x, axis, by):
    count = lax.axis_size(axis)
    pairs = [(i, i + by) for i in range(count) if 0 <= i + by < count]
    return lax.ppermute(x, axis, pairs)


def pair_kernel(group, heads, accumulate, sc_ref, q_ref, do_ref, k_ref, v_ref, lse_ref, dl_ref, *rest):
    if accumulate:
        dq_in_ref, dq_ref, dk_ref, dv_ref = rest
    else:
        dq_ref, dk_ref, dv_ref = rest
    rows = q_ref.shape[0]
    cols = k_ref.shape[0]
    qs = sc_ref[0]
    ks = sc_ref[1]
    vc = sc_ref[2]
    j = lax.broadcasted_iota(jnp.int32, (cols, rows), 0) + ks
    i = lax.broadcasted_iota(jnp.int32, (cols, rows), 1) + qs
    live = (j <= i) & (i - j < WINDOW) & (j >= 0) & (i < vc) & (j < vc)
    nt = (((1,), (1,)), ((), ()))
    tn = (((0,), (0,)), ((), ()))
    for c in range(heads):
        ksl = slice(c * HEAD_SIZE, (c + 1) * HEAD_SIZE)
        k = k_ref[:, ksl]
        v = v_ref[:, ksl]
        dk = jnp.zeros((cols, HEAD_SIZE), jnp.float32)
        dv = jnp.zeros((cols, HEAD_SIZE), jnp.float32)
        for g in range(group):
            hq = c * group + g
            sl = slice(hq * HEAD_SIZE, (hq + 1) * HEAD_SIZE)
            q = q_ref[:, sl]
            do = do_ref[:, sl]
            lse = lse_ref[c, g : g + 1, :]
            dl = dl_ref[c, g : g + 1, :]
            s = lax.dot_general(k, q, nt, preferred_element_type=jnp.float32) * score_scale
            p = jnp.where(live, jnp.exp(s - lse), 0.0)
            dp = lax.dot_general(v, do, nt, preferred_element_type=jnp.float32)
            ds = (p * (dp - dl)).astype(jnp.bfloat16)
            pb = p.astype(jnp.bfloat16)
            dv = dv + jnp.dot(pb, do, preferred_element_type=jnp.float32)
            dk = dk + jnp.dot(ds, q, preferred_element_type=jnp.float32)
            dq = lax.dot_general(ds, k, tn, preferred_element_type=jnp.float32) * score_scale
            if accumulate:
                dq = dq + dq_in_ref[:, sl]
            dq_ref[:, sl] = dq
        dk_ref[:, ksl] = (dk * score_scale).astype(dk_ref.dtype)
        dv_ref[:, ksl] = dv.astype(dv_ref.dtype)


def pair_grads(scalars, q, do, k, v, lse3, dl3, dq_in, kv_dtype):
    rows = q.shape[0]
    cols = k.shape[0]
    group = QUERY_HEADS // KEY_VALUE_HEADS
    accumulate = dq_in is not None
    heads = HEADS_PER_STEP
    qspec = pl.BlockSpec((rows, heads * group * HEAD_SIZE), lambda h, sc: (0, h))
    kspec = pl.BlockSpec((cols, heads * HEAD_SIZE), lambda h, sc: (0, h))
    sspec = pl.BlockSpec((heads, group, rows), lambda h, sc: (h, 0, 0))
    in_specs = [qspec, qspec, kspec, kspec, sspec, sspec]
    args = [q, do, k, v, lse3, dl3]
    if accumulate:
        in_specs.append(qspec)
        args.append(dq_in)
    out_shape = (
        jax.ShapeDtypeStruct((rows, QUERY_HEADS * HEAD_SIZE), jnp.float32),
        jax.ShapeDtypeStruct((cols, KEY_VALUE_HEADS * HEAD_SIZE), kv_dtype),
        jax.ShapeDtypeStruct((cols, KEY_VALUE_HEADS * HEAD_SIZE), kv_dtype),
    )
    flops = 5 * 2 * rows * cols * HEAD_SIZE * QUERY_HEADS
    nbytes = 2 * (2 * q.size + 2 * k.size) + 4 * q.size * (2 if accumulate else 1) + 2 * 2 * k.size * jnp.dtype(kv_dtype).itemsize
    return pl.pallas_call(
        functools.partial(pair_kernel, group, heads, accumulate),
        out_shape=out_shape,
        grid_spec=pltpu.PrefetchScalarGridSpec(
            num_scalar_prefetch=1,
            grid=(KEY_VALUE_HEADS // heads,),
            in_specs=in_specs,
            out_specs=[qspec, kspec, kspec],
        ),
        input_output_aliases=({7: 0} if accumulate else {}),
        cost_estimate=pl.CostEstimate(
            flops=flops, transcendentals=rows * cols * QUERY_HEADS, bytes_accessed=int(nbytes)
        ),
    )(scalars, *args)


def sent_by(x, axis, pairs):
    return lax.ppermute(x, axis, pairs)


def local(
    queries,
    stored_keys,
    stored_values,
    stored_output,
    output_cotangent,
    score_logsumexp,
    valid_count,
):
    tokens_here = queries.shape[0]
    blocks = WINDOW // tokens_here
    group = QUERY_HEADS // KEY_VALUE_HEADS
    count = lax.axis_size("seq")
    shard = lax.axis_index("seq")
    row = ROW_DEVICES
    kv = (stored_keys, stored_values)
    far = passed_along(kv, "seq", blocks)
    near = sent_by(kv, "seq", [(i, i + 1) for i in range(count - 1) if i % row != row - 1])
    handed = sent_by(far, "seq", [(i, i - row + 1) for i in range(row, count) if i % row == row - 1])
    halos = {blocks: far, 1: (near[0] + handed[0], near[1] + handed[1])}
    for distance in range(2, blocks):
        halos[distance] = passed_along(kv, "seq", distance)
    limit = valid_count[0]

    delta = jnp.sum(
        (output_cotangent.astype(jnp.float32) * stored_output.astype(jnp.float32)).reshape(
            tokens_here, QUERY_HEADS, HEAD_SIZE
        ),
        -1,
    )
    dl3 = delta.T.reshape(KEY_VALUE_HEADS, group, tokens_here)
    lse3 = score_logsumexp.reshape(KEY_VALUE_HEADS, group, tokens_here)
    qstart = shard * tokens_here

    def scalars_for(distance):
        return jnp.stack([qstart, qstart - distance * tokens_here, limit]).astype(jnp.int32)

    dq, key_grad, value_grad = pair_grads(
        scalars_for(0), queries, output_cotangent, stored_keys, stored_values, lse3, dl3, None, jnp.float32
    )
    handed_back = None
    for distance in PAIR_ORDER:
        k_far, v_far = halos[distance]
        dq, dk_part, dv_part = pair_grads(
            scalars_for(distance),
            queries,
            output_cotangent,
            k_far,
            v_far,
            lse3,
            dl3,
            dq,
            jnp.bfloat16,
        )
        if distance == 1:
            arrived = sent_by(
                (dk_part, dv_part), "seq", [(i, i - 1) for i in range(1, count) if i % row != 0]
            )
            handed_back = sent_by(
                (dk_part, dv_part), "seq", [(i, i + row - 1) for i in range(row, count) if i % row == 0]
            )
        else:
            if distance == blocks:
                dk_part = (dk_part.astype(jnp.float32) + handed_back[0].astype(jnp.float32)).astype(jnp.bfloat16)
                dv_part = (dv_part.astype(jnp.float32) + handed_back[1].astype(jnp.float32)).astype(jnp.bfloat16)
            arrived = passed_along((dk_part, dv_part), "seq", -distance)
        key_grad = key_grad + arrived[0].astype(jnp.float32)
        value_grad = value_grad + arrived[1].astype(jnp.float32)
    return (dq, key_grad, value_grad)


def solution(mesh):
    placed = (
        P(("grp", "seq"), None),
        P(("grp", "seq"), None),
        P(("grp", "seq"), None),
        P(("grp", "seq"), None),
        P(("grp", "seq"), None),
        P(None, ("grp", "seq")),
        P("grp"),
    )

    return jax.shard_map(
        local,
        mesh=mesh,
        in_specs=placed,
        out_specs=(P(("grp", "seq"), None), P(("grp", "seq"), None), P(("grp", "seq"), None)),
        check_vma=False,
    )
```

```python
import functools

import jax
import jax.numpy as jnp
from jax import lax
from jax.experimental import pallas as pl
from jax.experimental.pallas import tpu as pltpu
from jax.sharding import PartitionSpec as P


QUERY_HEADS = 32
KEY_VALUE_HEADS = 16
HEAD_SIZE = 128
WINDOW = 1024
HEADS_PER_STEP = 4
ROW_DEVICES = 4
PAIR_ORDER = (4, 1, 2, 3)


score_scale = 168.0 ** (-0.5)


def passed_along(x, axis, by):
    count = lax.axis_size(axis)
    pairs = [(i, i + by) for i in range(count) if 0 <= i + by < count]
    return lax.ppermute(x, axis, pairs)


def pair_kernel(group, heads, accumulate, sc_ref, q_ref, do_ref, k_ref, v_ref, lse_ref, dl_ref, *rest):
    if accumulate:
        dq_in_ref, dq_ref, dk_ref, dv_ref = rest
    else:
        dq_ref, dk_ref, dv_ref = rest
    rows = q_ref.shape[0]
    cols = k_ref.shape[0]
    qs = sc_ref[0]
    ks = sc_ref[1]
    vc = sc_ref[2]
    j = lax.broadcasted_iota(jnp.int32, (cols, rows), 0) + ks
    i = lax.broadcasted_iota(jnp.int32, (cols, rows), 1) + qs
    live = (j <= i) & (i - j < WINDOW) & (j >= 0) & (i < vc) & (j < vc)
    nt = (((1,), (1,)), ((), ()))
    tn = (((0,), (0,)), ((), ()))
    for c in range(heads):
        ksl = slice(c * HEAD_SIZE, (c + 1) * HEAD_SIZE)
        k = k_ref[:, ksl]
        v = v_ref[:, ksl]
        dk = jnp.zeros((cols, HEAD_SIZE), jnp.float32)
        dv = jnp.zeros((cols, HEAD_SIZE), jnp.float32)
        for g in range(group):
            hq = c * group + g
            sl = slice(hq * HEAD_SIZE, (hq + 1) * HEAD_SIZE)
            q = q_ref[:, sl]
            do = do_ref[:, sl]
            lse = lse_ref[c, g : g + 1, :]
            dl = dl_ref[c, g : g + 1, :]
            s = lax.dot_general(k, q, nt, preferred_element_type=jnp.float32) * score_scale
            p = jnp.where(live, jnp.exp(s - lse), 0.0)
            dp = lax.dot_general(v, do, nt, preferred_element_type=jnp.float32)
            ds = (p * (dp - dl)).astype(jnp.bfloat16)
            pb = p.astype(jnp.bfloat16)
            dv = dv + jnp.dot(pb, do, preferred_element_type=jnp.float32)
            dk = dk + jnp.dot(ds, q, preferred_element_type=jnp.float32)
            dq = lax.dot_general(ds, k, tn, preferred_element_type=jnp.float32) * score_scale
            if accumulate:
                dq = dq + dq_in_ref[:, sl]
            dq_ref[:, sl] = dq
        dk_ref[:, ksl] = (dk * score_scale).astype(dk_ref.dtype)
        dv_ref[:, ksl] = dv.astype(dv_ref.dtype)


def pair_grads(scalars, q, do, k, v, lse3, dl3, dq_in, kv_dtype):
    rows = q.shape[0]
    cols = k.shape[0]
    group = QUERY_HEADS // KEY_VALUE_HEADS
    accumulate = dq_in is not None
    heads = HEADS_PER_STEP
    qspec = pl.BlockSpec((rows, heads * group * HEAD_SIZE), lambda h, sc: (0, h))
    kspec = pl.BlockSpec((cols, heads * HEAD_SIZE), lambda h, sc: (0, h))
    sspec = pl.BlockSpec((heads, group, rows), lambda h, sc: (h, 0, 0))
    in_specs = [qspec, qspec, kspec, kspec, sspec, sspec]
    args = [q, do, k, v, lse3, dl3]
    if accumulate:
        in_specs.append(qspec)
        args.append(dq_in)
    out_shape = (
        jax.ShapeDtypeStruct((rows, QUERY_HEADS * HEAD_SIZE), jnp.float32),
        jax.ShapeDtypeStruct((cols, KEY_VALUE_HEADS * HEAD_SIZE), kv_dtype),
        jax.ShapeDtypeStruct((cols, KEY_VALUE_HEADS * HEAD_SIZE), kv_dtype),
    )
    flops = 5 * 2 * rows * cols * HEAD_SIZE * QUERY_HEADS
    nbytes = 2 * (2 * q.size + 2 * k.size) + 4 * q.size * (2 if accumulate else 1) + 2 * 2 * k.size * jnp.dtype(kv_dtype).itemsize
    return pl.pallas_call(
        functools.partial(pair_kernel, group, heads, accumulate),
        out_shape=out_shape,
        grid_spec=pltpu.PrefetchScalarGridSpec(
            num_scalar_prefetch=1,
            grid=(KEY_VALUE_HEADS // heads,),
            in_specs=in_specs,
            out_specs=[qspec, kspec, kspec],
        ),
        input_output_aliases=({7: 0} if accumulate else {}),
        cost_estimate=pl.CostEstimate(
            flops=flops, transcendentals=rows * cols * QUERY_HEADS, bytes_accessed=int(nbytes)
        ),
    )(scalars, *args)


def sent_by(x, axis, pairs):
    return lax.ppermute(x, axis, pairs)


def local(
    queries,
    stored_keys,
    stored_values,
    stored_output,
    output_cotangent,
    score_logsumexp,
    valid_count,
):
    tokens_here = queries.shape[0]
    blocks = WINDOW // tokens_here
    group = QUERY_HEADS // KEY_VALUE_HEADS
    count = lax.axis_size("seq")
    shard = lax.axis_index("seq")
    row = ROW_DEVICES
    kv = (stored_keys, stored_values)
    assert blocks == row
    far = passed_along(kv, "seq", blocks)
    halos = {blocks: far}
    for distance in range(1, blocks):
        direct = sent_by(
            kv, "seq", [(i, i + distance) for i in range(count) if i % row + distance < row]
        )
        relayed = sent_by(far, "seq", [(i, i - row + distance) for i in range(row, count) if i % row >= row - distance])
        halos[distance] = (direct[0] + relayed[0], direct[1] + relayed[1])
    limit = valid_count[0]

    delta = jnp.sum(
        (output_cotangent.astype(jnp.float32) * stored_output.astype(jnp.float32)).reshape(
            tokens_here, QUERY_HEADS, HEAD_SIZE
        ),
        -1,
    )
    dl3 = delta.T.reshape(KEY_VALUE_HEADS, group, tokens_here)
    lse3 = score_logsumexp.reshape(KEY_VALUE_HEADS, group, tokens_here)
    qstart = shard * tokens_here

    def scalars_for(distance):
        return jnp.stack([qstart, qstart - distance * tokens_here, limit]).astype(jnp.int32)

    dq, key_grad, value_grad = pair_grads(
        scalars_for(0), queries, output_cotangent, stored_keys, stored_values, lse3, dl3, None, jnp.float32
    )
    merged = []
    far_part = None
    for distance in PAIR_ORDER:
        k_far, v_far = halos[distance]
        dq, dk_part, dv_part = pair_grads(
            scalars_for(distance),
            queries,
            output_cotangent,
            k_far,
            v_far,
            lse3,
            dl3,
            dq,
            jnp.bfloat16,
        )
        if distance == blocks:
            far_part = (dk_part, dv_part)
            continue
        arrived = sent_by((dk_part, dv_part), "seq", [(i, i - distance) for i in range(count) if i % row >= distance])
        merged.append(
            sent_by((dk_part, dv_part), "seq", [(i, i + row - distance) for i in range(count) if i % row < distance])
        )
        key_grad = key_grad + arrived[0].astype(jnp.float32)
        value_grad = value_grad + arrived[1].astype(jnp.float32)
    dk_far = far_part[0].astype(jnp.float32)
    dv_far = far_part[1].astype(jnp.float32)
    for part in merged:
        dk_far = dk_far + part[0].astype(jnp.float32)
        dv_far = dv_far + part[1].astype(jnp.float32)
    arrived = passed_along((dk_far.astype(jnp.bfloat16), dv_far.astype(jnp.bfloat16)), "seq", -blocks)
    key_grad = key_grad + arrived[0].astype(jnp.float32)
    value_grad = value_grad + arrived[1].astype(jnp.float32)
    return (dq, key_grad, value_grad)


def solution(mesh):
    placed = (
        P(("grp", "seq"), None),
        P(("grp", "seq"), None),
        P(("grp", "seq"), None),
        P(("grp", "seq"), None),
        P(("grp", "seq"), None),
        P(None, ("grp", "seq")),
        P("grp"),
    )

    return jax.shard_map(
        local,
        mesh=mesh,
        in_specs=placed,
        out_specs=(P(("grp", "seq"), None), P(("grp", "seq"), None), P(("grp", "seq"), None)),
        check_vma=False,
    )
```

```python
import functools

import jax
import jax.numpy as jnp
from jax import lax
from jax.experimental import pallas as pl
from jax.experimental.pallas import tpu as pltpu
from jax.sharding import PartitionSpec as P


QUERY_HEADS = 32
KEY_VALUE_HEADS = 16
HEAD_SIZE = 128
WINDOW = 1024
HEADS_PER_STEP = 4
ROW_DEVICES = 4
PAIR_ORDER = (4, 1, 2, 3)


score_scale = 168.0 ** (-0.5)


def passed_along(x, axis, by):
    count = lax.axis_size(axis)
    pairs = [(i, i + by) for i in range(count) if 0 <= i + by < count]
    return lax.ppermute(x, axis, pairs)


def pair_kernel(group, heads, accumulate, parts, sc_ref, q_ref, do_ref, *refs):
    k_refs = refs[:parts]
    v_refs = refs[parts : 2 * parts]
    lse_ref, dl_ref = refs[2 * parts : 2 * parts + 2]
    rest = refs[2 * parts + 2 :]
    k_ref = k_refs[0]
    if accumulate:
        dq_in_ref, dq_ref, dk_ref, dv_ref = rest
    else:
        dq_ref, dk_ref, dv_ref = rest
    rows = q_ref.shape[0]
    cols = k_ref.shape[0]
    qs = sc_ref[0]
    ks = sc_ref[1]
    vc = sc_ref[2]
    j = lax.broadcasted_iota(jnp.int32, (cols, rows), 0) + ks
    i = lax.broadcasted_iota(jnp.int32, (cols, rows), 1) + qs
    live = (j <= i) & (i - j < WINDOW) & (j >= 0) & (i < vc) & (j < vc)
    nt = (((1,), (1,)), ((), ()))
    tn = (((0,), (0,)), ((), ()))
    for c in range(heads):
        ksl = slice(c * HEAD_SIZE, (c + 1) * HEAD_SIZE)
        k = k_refs[0][:, ksl]
        v = v_refs[0][:, ksl]
        for extra in range(1, parts):
            k = k + k_refs[extra][:, ksl]
            v = v + v_refs[extra][:, ksl]
        dk = jnp.zeros((cols, HEAD_SIZE), jnp.float32)
        dv = jnp.zeros((cols, HEAD_SIZE), jnp.float32)
        for g in range(group):
            hq = c * group + g
            sl = slice(hq * HEAD_SIZE, (hq + 1) * HEAD_SIZE)
            q = q_ref[:, sl]
            do = do_ref[:, sl]
            lse = lse_ref[c, g : g + 1, :]
            dl = dl_ref[c, g : g + 1, :]
            s = lax.dot_general(k, q, nt, preferred_element_type=jnp.float32) * score_scale
            p = jnp.where(live, jnp.exp(s - lse), 0.0)
            dp = lax.dot_general(v, do, nt, preferred_element_type=jnp.float32)
            ds = (p * (dp - dl)).astype(jnp.bfloat16)
            pb = p.astype(jnp.bfloat16)
            dv = dv + jnp.dot(pb, do, preferred_element_type=jnp.float32)
            dk = dk + jnp.dot(ds, q, preferred_element_type=jnp.float32)
            dq = lax.dot_general(ds, k, tn, preferred_element_type=jnp.float32) * score_scale
            if accumulate:
                dq = dq + dq_in_ref[:, sl]
            dq_ref[:, sl] = dq
        dk_ref[:, ksl] = (dk * score_scale).astype(dk_ref.dtype)
        dv_ref[:, ksl] = dv.astype(dv_ref.dtype)


def pair_grads(scalars, q, do, k, v, lse3, dl3, dq_in, kv_dtype):
    k = tuple(k) if isinstance(k, (tuple, list)) else (k,)
    v = tuple(v) if isinstance(v, (tuple, list)) else (v,)
    parts = len(k)
    rows = q.shape[0]
    cols = k[0].shape[0]
    group = QUERY_HEADS // KEY_VALUE_HEADS
    accumulate = dq_in is not None
    heads = HEADS_PER_STEP
    qspec = pl.BlockSpec((rows, heads * group * HEAD_SIZE), lambda h, sc: (0, h))
    kspec = pl.BlockSpec((cols, heads * HEAD_SIZE), lambda h, sc: (0, h))
    sspec = pl.BlockSpec((heads, group, rows), lambda h, sc: (h, 0, 0))
    in_specs = [qspec, qspec] + [kspec] * (2 * parts) + [sspec, sspec]
    args = [q, do, *k, *v, lse3, dl3]
    if accumulate:
        in_specs.append(qspec)
        args.append(dq_in)
    out_shape = (
        jax.ShapeDtypeStruct((rows, QUERY_HEADS * HEAD_SIZE), jnp.float32),
        jax.ShapeDtypeStruct((cols, KEY_VALUE_HEADS * HEAD_SIZE), kv_dtype),
        jax.ShapeDtypeStruct((cols, KEY_VALUE_HEADS * HEAD_SIZE), kv_dtype),
    )
    flops = 5 * 2 * rows * cols * HEAD_SIZE * QUERY_HEADS
    nbytes = 2 * (2 * q.size + 2 * parts * k[0].size) + 4 * q.size * (2 if accumulate else 1) + 2 * 2 * k[0].size * jnp.dtype(kv_dtype).itemsize
    return pl.pallas_call(
        functools.partial(pair_kernel, group, heads, accumulate, parts),
        out_shape=out_shape,
        grid_spec=pltpu.PrefetchScalarGridSpec(
            num_scalar_prefetch=1,
            grid=(KEY_VALUE_HEADS // heads,),
            in_specs=in_specs,
            out_specs=[qspec, kspec, kspec],
        ),
        input_output_aliases=({5 + 2 * parts: 0} if accumulate else {}),
        cost_estimate=pl.CostEstimate(
            flops=flops, transcendentals=rows * cols * QUERY_HEADS, bytes_accessed=int(nbytes)
        ),
    )(scalars, *args)


def sent_by(x, axis, pairs):
    return lax.ppermute(x, axis, pairs)


def local(
    queries,
    stored_keys,
    stored_values,
    stored_output,
    output_cotangent,
    score_logsumexp,
    valid_count,
):
    tokens_here = queries.shape[0]
    blocks = WINDOW // tokens_here
    group = QUERY_HEADS // KEY_VALUE_HEADS
    count = lax.axis_size("seq")
    shard = lax.axis_index("seq")
    row = ROW_DEVICES
    kv = (stored_keys, stored_values)
    assert blocks == row
    far = passed_along(kv, "seq", blocks)
    halos = {blocks: far}
    for distance in range(1, blocks):
        direct = sent_by(
            kv, "seq", [(i, i + distance) for i in range(count) if i % row + distance < row]
        )
        relayed = sent_by(
            far,
            "seq",
            [(i, i - row + distance) for i in range(row, count) if i % row >= row - distance],
        )
        halos[distance] = ((direct[0], relayed[0]), (direct[1], relayed[1]))
    limit = valid_count[0]

    delta = jnp.sum(
        (output_cotangent.astype(jnp.float32) * stored_output.astype(jnp.float32)).reshape(
            tokens_here, QUERY_HEADS, HEAD_SIZE
        ),
        -1,
    )
    dl3 = delta.T.reshape(KEY_VALUE_HEADS, group, tokens_here)
    lse3 = score_logsumexp.reshape(KEY_VALUE_HEADS, group, tokens_here)
    qstart = shard * tokens_here

    def scalars_for(distance):
        return jnp.stack([qstart, qstart - distance * tokens_here, limit]).astype(jnp.int32)

    dq, key_grad, value_grad = pair_grads(
        scalars_for(0), queries, output_cotangent, stored_keys, stored_values, lse3, dl3, None, jnp.float32
    )
    merged = []
    far_part = None
    for distance in PAIR_ORDER:
        k_far, v_far = halos[distance]
        dq, dk_part, dv_part = pair_grads(
            scalars_for(distance),
            queries,
            output_cotangent,
            k_far,
            v_far,
            lse3,
            dl3,
            dq,
            jnp.bfloat16,
        )
        if distance == blocks:
            far_part = (dk_part, dv_part)
            continue
        if distance == PAIR_ORDER[-1]:
            arrived = passed_along((dk_part, dv_part), "seq", -distance)
            key_grad = key_grad + arrived[0].astype(jnp.float32)
            value_grad = value_grad + arrived[1].astype(jnp.float32)
            continue
        arrived = sent_by(
            (dk_part, dv_part), "seq", [(i, i - distance) for i in range(count) if i % row >= distance]
        )
        merged.append(
            sent_by(
                (dk_part, dv_part),
                "seq",
                [(i, i + row - distance) for i in range(count) if i % row < distance],
            )
        )
        key_grad = key_grad + arrived[0].astype(jnp.float32)
        value_grad = value_grad + arrived[1].astype(jnp.float32)
    dk_far = far_part[0].astype(jnp.float32)
    dv_far = far_part[1].astype(jnp.float32)
    for part in merged:
        dk_far = dk_far + part[0].astype(jnp.float32)
        dv_far = dv_far + part[1].astype(jnp.float32)
    arrived = passed_along((dk_far.astype(jnp.bfloat16), dv_far.astype(jnp.bfloat16)), "seq", -blocks)
    key_grad = key_grad + arrived[0].astype(jnp.float32)
    value_grad = value_grad + arrived[1].astype(jnp.float32)
    return (dq, key_grad, value_grad)


def solution(mesh):
    placed = (
        P(("grp", "seq"), None),
        P(("grp", "seq"), None),
        P(("grp", "seq"), None),
        P(("grp", "seq"), None),
        P(("grp", "seq"), None),
        P(None, ("grp", "seq")),
        P("grp"),
    )

    return jax.shard_map(
        local,
        mesh=mesh,
        in_specs=placed,
        out_specs=(P(("grp", "seq"), None), P(("grp", "seq"), None), P(("grp", "seq"), None)),
        check_vma=False,
    )
```

```python
import functools

import jax
import jax.numpy as jnp
from jax import lax
from jax.experimental import pallas as pl
from jax.experimental.pallas import tpu as pltpu
from jax.sharding import PartitionSpec as P


QUERY_HEADS = 32
KEY_VALUE_HEADS = 16
HEAD_SIZE = 128
WINDOW = 1024
HEADS_PER_STEP = 4
ROW_DEVICES = 4
PAIR_ORDER = (1, 3, 2, 4)


score_scale = 168.0 ** (-0.5)


def passed_along(x, axis, by):
    count = lax.axis_size(axis)
    pairs = [(i, i + by) for i in range(count) if 0 <= i + by < count]
    return lax.ppermute(x, axis, pairs)


def pair_kernel(group, heads, accumulate, parts, sc_ref, q_ref, do_ref, *refs):
    k_refs = refs[:parts]
    v_refs = refs[parts : 2 * parts]
    lse_ref, dl_ref = refs[2 * parts : 2 * parts + 2]
    rest = refs[2 * parts + 2 :]
    k_ref = k_refs[0]
    if accumulate:
        dq_in_ref, dq_ref, dk_ref, dv_ref = rest
    else:
        dq_ref, dk_ref, dv_ref = rest
    rows = q_ref.shape[0]
    cols = k_ref.shape[0]
    qs = sc_ref[0]
    ks = sc_ref[1]
    vc = sc_ref[2]
    j = lax.broadcasted_iota(jnp.int32, (cols, rows), 0) + ks
    i = lax.broadcasted_iota(jnp.int32, (cols, rows), 1) + qs
    live = (j <= i) & (i - j < WINDOW) & (j >= 0) & (i < vc) & (j < vc)
    nt = (((1,), (1,)), ((), ()))
    tn = (((0,), (0,)), ((), ()))
    for c in range(heads):
        ksl = slice(c * HEAD_SIZE, (c + 1) * HEAD_SIZE)
        k = k_refs[0][:, ksl]
        v = v_refs[0][:, ksl]
        for extra in range(1, parts):
            k = k + k_refs[extra][:, ksl]
            v = v + v_refs[extra][:, ksl]
        dk = jnp.zeros((cols, HEAD_SIZE), jnp.float32)
        dv = jnp.zeros((cols, HEAD_SIZE), jnp.float32)
        for g in range(group):
            hq = c * group + g
            sl = slice(hq * HEAD_SIZE, (hq + 1) * HEAD_SIZE)
            q = q_ref[:, sl]
            do = do_ref[:, sl]
            lse = lse_ref[c, g : g + 1, :]
            dl = dl_ref[c, g : g + 1, :]
            s = lax.dot_general(k, q, nt, preferred_element_type=jnp.float32) * score_scale
            p = jnp.where(live, jnp.exp(s - lse), 0.0)
            dp = lax.dot_general(v, do, nt, preferred_element_type=jnp.float32)
            ds = (p * (dp - dl)).astype(jnp.bfloat16)
            pb = p.astype(jnp.bfloat16)
            dv = dv + jnp.dot(pb, do, preferred_element_type=jnp.float32)
            dk = dk + jnp.dot(ds, q, preferred_element_type=jnp.float32)
            dq = lax.dot_general(ds, k, tn, preferred_element_type=jnp.float32) * score_scale
            if accumulate:
                dq = dq + dq_in_ref[:, sl]
            dq_ref[:, sl] = dq
        dk_ref[:, ksl] = (dk * score_scale).astype(dk_ref.dtype)
        dv_ref[:, ksl] = dv.astype(dv_ref.dtype)


def pair_grads(scalars, q, do, k, v, lse3, dl3, dq_in, kv_dtype):
    k = tuple(k) if isinstance(k, (tuple, list)) else (k,)
    v = tuple(v) if isinstance(v, (tuple, list)) else (v,)
    parts = len(k)
    rows = q.shape[0]
    cols = k[0].shape[0]
    group = QUERY_HEADS // KEY_VALUE_HEADS
    accumulate = dq_in is not None
    heads = HEADS_PER_STEP
    qspec = pl.BlockSpec((rows, heads * group * HEAD_SIZE), lambda h, sc: (0, h))
    kspec = pl.BlockSpec((cols, heads * HEAD_SIZE), lambda h, sc: (0, h))
    sspec = pl.BlockSpec((heads, group, rows), lambda h, sc: (h, 0, 0))
    in_specs = [qspec, qspec] + [kspec] * (2 * parts) + [sspec, sspec]
    args = [q, do, *k, *v, lse3, dl3]
    if accumulate:
        in_specs.append(qspec)
        args.append(dq_in)
    out_shape = (
        jax.ShapeDtypeStruct((rows, QUERY_HEADS * HEAD_SIZE), jnp.float32),
        jax.ShapeDtypeStruct((cols, KEY_VALUE_HEADS * HEAD_SIZE), kv_dtype),
        jax.ShapeDtypeStruct((cols, KEY_VALUE_HEADS * HEAD_SIZE), kv_dtype),
    )
    flops = 5 * 2 * rows * cols * HEAD_SIZE * QUERY_HEADS
    nbytes = 2 * (2 * q.size + 2 * parts * k[0].size) + 4 * q.size * (2 if accumulate else 1) + 2 * 2 * k[0].size * jnp.dtype(kv_dtype).itemsize
    return pl.pallas_call(
        functools.partial(pair_kernel, group, heads, accumulate, parts),
        out_shape=out_shape,
        grid_spec=pltpu.PrefetchScalarGridSpec(
            num_scalar_prefetch=1,
            grid=(KEY_VALUE_HEADS // heads,),
            in_specs=in_specs,
            out_specs=[qspec, kspec, kspec],
        ),
        input_output_aliases=({5 + 2 * parts: 0} if accumulate else {}),
        cost_estimate=pl.CostEstimate(
            flops=flops, transcendentals=rows * cols * QUERY_HEADS, bytes_accessed=int(nbytes)
        ),
    )(scalars, *args)


def sent_by(x, axis, pairs):
    return lax.ppermute(x, axis, pairs)


def local(
    queries,
    stored_keys,
    stored_values,
    stored_output,
    output_cotangent,
    score_logsumexp,
    valid_count,
):
    tokens_here = queries.shape[0]
    blocks = WINDOW // tokens_here
    group = QUERY_HEADS // KEY_VALUE_HEADS
    count = lax.axis_size("seq")
    shard = lax.axis_index("seq")
    row = ROW_DEVICES
    kv = (stored_keys, stored_values)
    assert blocks == row
    far = passed_along(kv, "seq", blocks)
    near1 = sent_by(kv, "seq", [(i, i + 1) for i in range(count) if i % row < row - 1])
    relay1 = sent_by(far, "seq", [(i, i - row + 1) for i in range(row, count) if i % row == row - 1])
    near3 = sent_by(kv, "seq", [(i, i + row - 1) for i in range(count) if i % row == 0])
    relay3 = sent_by(far, "seq", [(i, i - 1) for i in range(row, count) if i % row >= 1])
    fwd2a = sent_by(near1, "seq", [(i, i + 1) for i in range(count) if 1 <= i % row <= row - 2])
    fwd2b = sent_by(relay3, "seq", [(i, i - 1) for i in range(row, count) if 1 <= i % row <= row - 2])
    halos = {
        blocks: far,
        1: ((near1[0], relay1[0]), (near1[1], relay1[1])),
        2: ((fwd2a[0], fwd2b[0]), (fwd2a[1], fwd2b[1])),
        3: ((near3[0], relay3[0]), (near3[1], relay3[1])),
    }
    limit = valid_count[0]

    delta = jnp.sum(
        (output_cotangent.astype(jnp.float32) * stored_output.astype(jnp.float32)).reshape(
            tokens_here, QUERY_HEADS, HEAD_SIZE
        ),
        -1,
    )
    dl3 = delta.T.reshape(KEY_VALUE_HEADS, group, tokens_here)
    lse3 = score_logsumexp.reshape(KEY_VALUE_HEADS, group, tokens_here)
    qstart = shard * tokens_here

    def scalars_for(distance):
        return jnp.stack([qstart, qstart - distance * tokens_here, limit]).astype(jnp.int32)

    dq, key_grad, value_grad = pair_grads(
        scalars_for(0), queries, output_cotangent, stored_keys, stored_values, lse3, dl3, None, jnp.float32
    )
    merged = []
    far_part = None
    for distance in PAIR_ORDER:
        k_far, v_far = halos[distance]
        dq, dk_part, dv_part = pair_grads(
            scalars_for(distance),
            queries,
            output_cotangent,
            k_far,
            v_far,
            lse3,
            dl3,
            dq,
            jnp.bfloat16,
        )
        if distance == blocks:
            far_part = (dk_part, dv_part)
            continue
        arrived = sent_by((dk_part, dv_part), "seq", [(i, i - distance) for i in range(count) if i % row >= distance])
        merged.append(
            sent_by((dk_part, dv_part), "seq", [(i, i + row - distance) for i in range(count) if i % row < distance])
        )
        key_grad = key_grad + arrived[0].astype(jnp.float32)
        value_grad = value_grad + arrived[1].astype(jnp.float32)
    dk_far = far_part[0].astype(jnp.float32)
    dv_far = far_part[1].astype(jnp.float32)
    for part in merged:
        dk_far = dk_far + part[0].astype(jnp.float32)
        dv_far = dv_far + part[1].astype(jnp.float32)
    arrived = passed_along((dk_far.astype(jnp.bfloat16), dv_far.astype(jnp.bfloat16)), "seq", -blocks)
    key_grad = key_grad + arrived[0].astype(jnp.float32)
    value_grad = value_grad + arrived[1].astype(jnp.float32)
    return (dq, key_grad, value_grad)


def solution(mesh):
    placed = (
        P(("grp", "seq"), None),
        P(("grp", "seq"), None),
        P(("grp", "seq"), None),
        P(("grp", "seq"), None),
        P(("grp", "seq"), None),
        P(None, ("grp", "seq")),
        P("grp"),
    )

    return jax.shard_map(
        local,
        mesh=mesh,
        in_specs=placed,
        out_specs=(P(("grp", "seq"), None), P(("grp", "seq"), None), P(("grp", "seq"), None)),
        check_vma=False,
    )
```

```python
import functools

import jax
import jax.numpy as jnp
from jax import lax
from jax.experimental import pallas as pl
from jax.experimental.pallas import tpu as pltpu
from jax.sharding import PartitionSpec as P


QUERY_HEADS = 32
KEY_VALUE_HEADS = 16
HEAD_SIZE = 128
WINDOW = 1024
HEADS_PER_STEP = 4
ROW_DEVICES = 4
PAIR_ORDER = (1, 3, 2, 4)


score_scale = 168.0 ** (-0.5)


def passed_along(x, axis, by):
    count = lax.axis_size(axis)
    pairs = [(i, i + by) for i in range(count) if 0 <= i + by < count]
    return lax.ppermute(x, axis, pairs)


def pair_kernel(group, heads, accumulate, parts, sc_ref, q_ref, do_ref, *refs):
    k_refs = refs[:parts]
    v_refs = refs[parts : 2 * parts]
    lse_ref, dl_ref = refs[2 * parts : 2 * parts + 2]
    rest = refs[2 * parts + 2 :]
    k_ref = k_refs[0]
    if accumulate:
        dq_in_ref, dq_ref, dk_ref, dv_ref = rest
    else:
        dq_ref, dk_ref, dv_ref = rest
    rows = q_ref.shape[0]
    cols = k_ref.shape[0]
    qs = sc_ref[0]
    ks = sc_ref[1]
    vc = sc_ref[2]
    j = lax.broadcasted_iota(jnp.int32, (cols, rows), 0) + ks
    i = lax.broadcasted_iota(jnp.int32, (cols, rows), 1) + qs
    live = (j <= i) & (i - j < WINDOW) & (j >= 0) & (i < vc) & (j < vc)
    nt = (((1,), (1,)), ((), ()))
    tn = (((0,), (0,)), ((), ()))
    for c in range(heads):
        ksl = slice(c * HEAD_SIZE, (c + 1) * HEAD_SIZE)
        k = k_refs[0][:, ksl]
        v = v_refs[0][:, ksl]
        for extra in range(1, parts):
            k = k + k_refs[extra][:, ksl]
            v = v + v_refs[extra][:, ksl]
        dk = jnp.zeros((cols, HEAD_SIZE), jnp.float32)
        dv = jnp.zeros((cols, HEAD_SIZE), jnp.float32)
        for g in range(group):
            hq = c * group + g
            sl = slice(hq * HEAD_SIZE, (hq + 1) * HEAD_SIZE)
            q = q_ref[:, sl]
            do = do_ref[:, sl]
            lse = lse_ref[c, g : g + 1, :]
            dl = dl_ref[c, g : g + 1, :]
            s = lax.dot_general(k, q, nt, preferred_element_type=jnp.float32) * score_scale
            p = jnp.where(live, jnp.exp(s - lse), 0.0)
            dp = lax.dot_general(v, do, nt, preferred_element_type=jnp.float32)
            ds = (p * (dp - dl)).astype(jnp.bfloat16)
            pb = p.astype(jnp.bfloat16)
            dv = dv + jnp.dot(pb, do, preferred_element_type=jnp.float32)
            dk = dk + jnp.dot(ds, q, preferred_element_type=jnp.float32)
            dq = lax.dot_general(ds, k, tn, preferred_element_type=jnp.float32) * score_scale
            if accumulate:
                dq = dq + dq_in_ref[:, sl]
            dq_ref[:, sl] = dq
        dk_ref[:, ksl] = (dk * score_scale).astype(dk_ref.dtype)
        dv_ref[:, ksl] = dv.astype(dv_ref.dtype)


def pair_grads(scalars, q, do, k, v, lse3, dl3, dq_in, kv_dtype):
    k = tuple(k) if isinstance(k, (tuple, list)) else (k,)
    v = tuple(v) if isinstance(v, (tuple, list)) else (v,)
    parts = len(k)
    rows = q.shape[0]
    cols = k[0].shape[0]
    group = QUERY_HEADS // KEY_VALUE_HEADS
    accumulate = dq_in is not None
    heads = HEADS_PER_STEP
    qspec = pl.BlockSpec((rows, heads * group * HEAD_SIZE), lambda h, sc: (0, h))
    kspec = pl.BlockSpec((cols, heads * HEAD_SIZE), lambda h, sc: (0, h))
    sspec = pl.BlockSpec((heads, group, rows), lambda h, sc: (h, 0, 0))
    in_specs = [qspec, qspec] + [kspec] * (2 * parts) + [sspec, sspec]
    args = [q, do, *k, *v, lse3, dl3]
    if accumulate:
        in_specs.append(qspec)
        args.append(dq_in)
    out_shape = (
        jax.ShapeDtypeStruct((rows, QUERY_HEADS * HEAD_SIZE), jnp.float32),
        jax.ShapeDtypeStruct((cols, KEY_VALUE_HEADS * HEAD_SIZE), kv_dtype),
        jax.ShapeDtypeStruct((cols, KEY_VALUE_HEADS * HEAD_SIZE), kv_dtype),
    )
    flops = 5 * 2 * rows * cols * HEAD_SIZE * QUERY_HEADS
    nbytes = 2 * (2 * q.size + 2 * parts * k[0].size) + 4 * q.size * (2 if accumulate else 1) + 2 * 2 * k[0].size * jnp.dtype(kv_dtype).itemsize
    return pl.pallas_call(
        functools.partial(pair_kernel, group, heads, accumulate, parts),
        out_shape=out_shape,
        grid_spec=pltpu.PrefetchScalarGridSpec(
            num_scalar_prefetch=1,
            grid=(KEY_VALUE_HEADS // heads,),
            in_specs=in_specs,
            out_specs=[qspec, kspec, kspec],
        ),
        input_output_aliases=({5 + 2 * parts: 0} if accumulate else {}),
        cost_estimate=pl.CostEstimate(
            flops=flops, transcendentals=rows * cols * QUERY_HEADS, bytes_accessed=int(nbytes)
        ),
    )(scalars, *args)


def sent_by(x, axis, pairs):
    return lax.ppermute(x, axis, pairs)


def local(
    queries,
    stored_keys,
    stored_values,
    stored_output,
    output_cotangent,
    score_logsumexp,
    valid_count,
):
    tokens_here = queries.shape[0]
    blocks = WINDOW // tokens_here
    group = QUERY_HEADS // KEY_VALUE_HEADS
    count = lax.axis_size("seq")
    shard = lax.axis_index("seq")
    row = ROW_DEVICES
    kv = (stored_keys, stored_values)
    assert blocks == row
    far = passed_along(kv, "seq", blocks)
    near1 = sent_by(kv, "seq", [(i, i + 1) for i in range(count) if i % row < row - 1])
    relay1 = sent_by(far, "seq", [(i, i - row + 1) for i in range(row, count) if i % row == row - 1])
    near3 = sent_by(kv, "seq", [(i, i + row - 1) for i in range(count) if i % row == 0])
    relay3 = sent_by(far, "seq", [(i, i - 1) for i in range(row, count) if i % row >= 1])
    fwd2a = sent_by(near1, "seq", [(i, i + 1) for i in range(count) if 1 <= i % row <= row - 2])
    fwd2b = sent_by(relay3, "seq", [(i, i - 1) for i in range(row, count) if 1 <= i % row <= row - 2])
    halos = {
        blocks: far,
        1: ((near1[0], relay1[0]), (near1[1], relay1[1])),
        2: ((fwd2a[0], fwd2b[0]), (fwd2a[1], fwd2b[1])),
        3: ((near3[0], relay3[0]), (near3[1], relay3[1])),
    }
    limit = valid_count[0]

    delta = jnp.sum(
        (output_cotangent.astype(jnp.float32) * stored_output.astype(jnp.float32)).reshape(
            tokens_here, QUERY_HEADS, HEAD_SIZE
        ),
        -1,
    )
    dl3 = delta.T.reshape(KEY_VALUE_HEADS, group, tokens_here)
    lse3 = score_logsumexp.reshape(KEY_VALUE_HEADS, group, tokens_here)
    qstart = shard * tokens_here

    def scalars_for(distance):
        return jnp.stack([qstart, qstart - distance * tokens_here, limit]).astype(jnp.int32)

    dq, key_grad, value_grad = pair_grads(
        scalars_for(0), queries, output_cotangent, stored_keys, stored_values, lse3, dl3, None, jnp.float32
    )
    merged = []
    far_part = None
    for distance in PAIR_ORDER:
        k_far, v_far = halos[distance]
        dq, dk_part, dv_part = pair_grads(
            scalars_for(distance),
            queries,
            output_cotangent,
            k_far,
            v_far,
            lse3,
            dl3,
            dq,
            jnp.bfloat16,
        )
        if distance == blocks:
            far_part = (dk_part, dv_part)
            continue
        got = sent_by(
            (dk_part, dv_part),
            "seq",
            [(i, i - distance) if i % row >= distance else (i, i + row - distance) for i in range(count)
             if (i - distance >= 0 if i % row >= distance else i + row - distance < count)],
        )
        direct = shard % row + distance < row
        zero = jnp.zeros((), jnp.bfloat16)
        merged.append((jnp.where(direct, zero, got[0]), jnp.where(direct, zero, got[1])))
        key_grad = key_grad + jnp.where(direct, got[0], zero).astype(jnp.float32)
        value_grad = value_grad + jnp.where(direct, got[1], zero).astype(jnp.float32)
    dk_far = far_part[0].astype(jnp.float32)
    dv_far = far_part[1].astype(jnp.float32)
    for part in merged:
        dk_far = dk_far + part[0].astype(jnp.float32)
        dv_far = dv_far + part[1].astype(jnp.float32)
    arrived = passed_along((dk_far.astype(jnp.bfloat16), dv_far.astype(jnp.bfloat16)), "seq", -blocks)
    key_grad = key_grad + arrived[0].astype(jnp.float32)
    value_grad = value_grad + arrived[1].astype(jnp.float32)
    return (dq, key_grad, value_grad)


def solution(mesh):
    placed = (
        P(("grp", "seq"), None),
        P(("grp", "seq"), None),
        P(("grp", "seq"), None),
        P(("grp", "seq"), None),
        P(("grp", "seq"), None),
        P(None, ("grp", "seq")),
        P("grp"),
    )

    return jax.shard_map(
        local,
        mesh=mesh,
        in_specs=placed,
        out_specs=(P(("grp", "seq"), None), P(("grp", "seq"), None), P(("grp", "seq"), None)),
        check_vma=False,
    )
```

```python
import functools

import jax
import jax.numpy as jnp
from jax import lax
from jax.experimental import pallas as pl
from jax.experimental.pallas import tpu as pltpu
from jax.sharding import PartitionSpec as P


QUERY_HEADS = 32
KEY_VALUE_HEADS = 16
HEAD_SIZE = 128
WINDOW = 1024
HEADS_PER_STEP = 2
ROW_DEVICES = 4
PAIR_ORDER = (1, 3, 4, 2)


score_scale = 168.0 ** (-0.5)


def passed_along(x, axis, by):
    count = lax.axis_size(axis)
    pairs = [(i, i + by) for i in range(count) if 0 <= i + by < count]
    return lax.ppermute(x, axis, pairs)


def pair_kernel(group, heads, accumulate, parts, sc_ref, q_ref, do_ref, *refs):
    k_refs = refs[:parts]
    v_refs = refs[parts : 2 * parts]
    lse_ref, dl_ref = refs[2 * parts : 2 * parts + 2]
    rest = refs[2 * parts + 2 :]
    k_ref = k_refs[0]
    if accumulate:
        dq_in_ref, dq_ref, dk_ref, dv_ref = rest
    else:
        dq_ref, dk_ref, dv_ref = rest
    rows = q_ref.shape[0]
    cols = k_ref.shape[0]
    qs = sc_ref[0]
    ks = sc_ref[1]
    vc = sc_ref[2]
    j = lax.broadcasted_iota(jnp.int32, (cols, rows), 0) + ks
    i = lax.broadcasted_iota(jnp.int32, (cols, rows), 1) + qs
    live = (j <= i) & (i - j < WINDOW) & (j >= 0) & (i < vc) & (j < vc)
    nt = (((1,), (1,)), ((), ()))
    tn = (((0,), (0,)), ((), ()))
    for c in range(heads):
        ksl = slice(c * HEAD_SIZE, (c + 1) * HEAD_SIZE)
        k = k_refs[0][:, ksl]
        v = v_refs[0][:, ksl]
        for extra in range(1, parts):
            k = k + k_refs[extra][:, ksl]
            v = v + v_refs[extra][:, ksl]
        dk = jnp.zeros((cols, HEAD_SIZE), jnp.float32)
        dv = jnp.zeros((cols, HEAD_SIZE), jnp.float32)
        for g in range(group):
            hq = c * group + g
            sl = slice(hq * HEAD_SIZE, (hq + 1) * HEAD_SIZE)
            q = q_ref[:, sl]
            do = do_ref[:, sl]
            lse = lse_ref[c, g : g + 1, :]
            dl = dl_ref[c, g : g + 1, :]
            s = lax.dot_general(k, q, nt, preferred_element_type=jnp.float32) * score_scale
            p = jnp.where(live, jnp.exp(s - lse), 0.0)
            dp = lax.dot_general(v, do, nt, preferred_element_type=jnp.float32)
            ds = (p * (dp - dl)).astype(jnp.bfloat16)
            pb = p.astype(jnp.bfloat16)
            dv = dv + jnp.dot(pb, do, preferred_element_type=jnp.float32)
            dk = dk + jnp.dot(ds, q, preferred_element_type=jnp.float32)
            dq = lax.dot_general(ds, k, tn, preferred_element_type=jnp.float32) * score_scale
            if accumulate:
                dq = dq + dq_in_ref[:, sl]
            dq_ref[:, sl] = dq
        dk_ref[:, ksl] = (dk * score_scale).astype(dk_ref.dtype)
        dv_ref[:, ksl] = dv.astype(dv_ref.dtype)


def pair_grads(scalars, q, do, k, v, lse3, dl3, dq_in, kv_dtype):
    k = tuple(k) if isinstance(k, (tuple, list)) else (k,)
    v = tuple(v) if isinstance(v, (tuple, list)) else (v,)
    parts = len(k)
    rows = q.shape[0]
    cols = k[0].shape[0]
    group = QUERY_HEADS // KEY_VALUE_HEADS
    accumulate = dq_in is not None
    heads = HEADS_PER_STEP
    qspec = pl.BlockSpec((rows, heads * group * HEAD_SIZE), lambda h, sc: (0, h))
    kspec = pl.BlockSpec((cols, heads * HEAD_SIZE), lambda h, sc: (0, h))
    sspec = pl.BlockSpec((heads, group, rows), lambda h, sc: (h, 0, 0))
    in_specs = [qspec, qspec] + [kspec] * (2 * parts) + [sspec, sspec]
    args = [q, do, *k, *v, lse3, dl3]
    if accumulate:
        in_specs.append(qspec)
        args.append(dq_in)
    out_shape = (
        jax.ShapeDtypeStruct((rows, QUERY_HEADS * HEAD_SIZE), jnp.float32),
        jax.ShapeDtypeStruct((cols, KEY_VALUE_HEADS * HEAD_SIZE), kv_dtype),
        jax.ShapeDtypeStruct((cols, KEY_VALUE_HEADS * HEAD_SIZE), kv_dtype),
    )
    flops = 5 * 2 * rows * cols * HEAD_SIZE * QUERY_HEADS
    nbytes = 2 * (2 * q.size + 2 * parts * k[0].size) + 4 * q.size * (2 if accumulate else 1) + 2 * 2 * k[0].size * jnp.dtype(kv_dtype).itemsize
    return pl.pallas_call(
        functools.partial(pair_kernel, group, heads, accumulate, parts),
        out_shape=out_shape,
        grid_spec=pltpu.PrefetchScalarGridSpec(
            num_scalar_prefetch=1,
            grid=(KEY_VALUE_HEADS // heads,),
            in_specs=in_specs,
            out_specs=[qspec, kspec, kspec],
        ),
        input_output_aliases=({5 + 2 * parts: 0} if accumulate else {}),
        cost_estimate=pl.CostEstimate(
            flops=flops, transcendentals=rows * cols * QUERY_HEADS, bytes_accessed=int(nbytes)
        ),
    )(scalars, *args)


def sent_by(x, axis, pairs):
    return lax.ppermute(x, axis, pairs)


def local(
    queries,
    stored_keys,
    stored_values,
    stored_output,
    output_cotangent,
    score_logsumexp,
    valid_count,
):
    tokens_here = queries.shape[0]
    blocks = WINDOW // tokens_here
    group = QUERY_HEADS // KEY_VALUE_HEADS
    count = lax.axis_size("seq")
    shard = lax.axis_index("seq")
    row = ROW_DEVICES
    kv = (stored_keys, stored_values)
    assert blocks == row
    far = passed_along(kv, "seq", blocks)
    near1 = sent_by(kv, "seq", [(i, i + 1) for i in range(count) if i % row < row - 1])
    relay1 = sent_by(far, "seq", [(i, i - row + 1) for i in range(row, count) if i % row == row - 1])
    near3 = sent_by(kv, "seq", [(i, i + row - 1) for i in range(count) if i % row == 0])
    relay3 = sent_by(far, "seq", [(i, i - 1) for i in range(row, count) if i % row >= 1])
    fwd2a = sent_by(near1, "seq", [(i, i + 1) for i in range(count) if 1 <= i % row <= row - 2])
    fwd2b = sent_by(relay3, "seq", [(i, i - 1) for i in range(row, count) if 1 <= i % row <= row - 2])
    halos = {
        blocks: far,
        1: ((near1[0], relay1[0]), (near1[1], relay1[1])),
        2: ((fwd2a[0], fwd2b[0]), (fwd2a[1], fwd2b[1])),
        3: ((near3[0], relay3[0]), (near3[1], relay3[1])),
    }
    limit = valid_count[0]

    delta = jnp.sum(
        (output_cotangent.astype(jnp.float32) * stored_output.astype(jnp.float32)).reshape(
            tokens_here, QUERY_HEADS, HEAD_SIZE
        ),
        -1,
    )
    dl3 = delta.T.reshape(KEY_VALUE_HEADS, group, tokens_here)
    lse3 = score_logsumexp.reshape(KEY_VALUE_HEADS, group, tokens_here)
    qstart = shard * tokens_here

    def scalars_for(distance):
        return jnp.stack([qstart, qstart - distance * tokens_here, limit]).astype(jnp.int32)

    dq, key_grad, value_grad = pair_grads(
        scalars_for(0), queries, output_cotangent, stored_keys, stored_values, lse3, dl3, None, jnp.float32
    )
    merged = []
    far_part = None
    for distance in PAIR_ORDER:
        k_far, v_far = halos[distance]
        dq, dk_part, dv_part = pair_grads(
            scalars_for(distance),
            queries,
            output_cotangent,
            k_far,
            v_far,
            lse3,
            dl3,
            dq,
            jnp.bfloat16,
        )
        if distance == blocks:
            far_part = (dk_part, dv_part)
            continue
        if distance == PAIR_ORDER[-1]:
            got = passed_along((dk_part, dv_part), "seq", -distance)
            key_grad = key_grad + got[0].astype(jnp.float32)
            value_grad = value_grad + got[1].astype(jnp.float32)
            continue
        got = sent_by(
            (dk_part, dv_part),
            "seq",
            [(i, i - distance) if i % row >= distance else (i, i + row - distance) for i in range(count)
             if (i - distance >= 0 if i % row >= distance else i + row - distance < count)],
        )
        direct = shard % row + distance < row
        zero = jnp.zeros((), jnp.bfloat16)
        merged.append((jnp.where(direct, zero, got[0]), jnp.where(direct, zero, got[1])))
        key_grad = key_grad + jnp.where(direct, got[0], zero).astype(jnp.float32)
        value_grad = value_grad + jnp.where(direct, got[1], zero).astype(jnp.float32)
    dk_far = far_part[0].astype(jnp.float32)
    dv_far = far_part[1].astype(jnp.float32)
    for part in merged:
        dk_far = dk_far + part[0].astype(jnp.float32)
        dv_far = dv_far + part[1].astype(jnp.float32)
    arrived = passed_along((dk_far.astype(jnp.bfloat16), dv_far.astype(jnp.bfloat16)), "seq", -blocks)
    key_grad = key_grad + arrived[0].astype(jnp.float32)
    value_grad = value_grad + arrived[1].astype(jnp.float32)
    return (dq, key_grad, value_grad)


def solution(mesh):
    placed = (
        P(("grp", "seq"), None),
        P(("grp", "seq"), None),
        P(("grp", "seq"), None),
        P(("grp", "seq"), None),
        P(("grp", "seq"), None),
        P(None, ("grp", "seq")),
        P("grp"),
    )

    return jax.shard_map(
        local,
        mesh=mesh,
        in_specs=placed,
        out_specs=(P(("grp", "seq"), None), P(("grp", "seq"), None), P(("grp", "seq"), None)),
        check_vma=False,
    )
```
